1024 devices in a mesh: context: 32 (over x, y, core), tensor: 32 (over z).
Axes of the slice: x: 4, y: 4, z: 32, core: 2. Of those that a mesh axis runs over, the one named last changes fastest.
Arguments:
- tokens_t: bfloat16 [6144, 8192], P('tensor', 'context'), may hold values from -6 to 6
- qkv_weight: bfloat16 [6144, 24576], P(None, 'tensor'), may hold values from -1.5309311 to 1.5309311, as said below
- prior_state: float32 [64, 128, 128], P('tensor'), may hold values from -192 to 192
- norm_gain: float32 [8192], P('tensor'), may hold values from 0.1 to 1.9
Outputs:
- mixed: bfloat16 [8192, 8192], P('context', 'tensor')
The draws below stay inside these ranges and needn't reach their ends.
Inputs may be any that keep to these rules, and one draw needn't show every extreme that they name: `qkv_weight`: column h * 3 * 128 + p * 128 + e projects onto feature e of head h, with p = 0, 1, 2 for query, key and value.
All inputs are finite; a program needn't handle non-finite values.
Results may differ from the reference program's by a relative error of at most 0.0034.
Values may be sent and summed in bfloat16 or wider, within the bound.
A program may use at most 32 MiB of HBM per device.

```python
import jax
import jax.numpy as jnp
from jax import lax

D = 6144
H = 64
HEAD = 128
GROUP = 256
TOKENS = 8192
N_CONTEXT = 32


def draw_qkv_weight(key, part):
    base = jnp.clip(jax.random.normal(key, (D, H, 3, HEAD), jnp.float32), -6.0, 6.0)
    head_pos = jnp.arange(H, dtype=jnp.float32) / max(H - 1, 1)
    top_scale = 10.0
    value_scale = top_scale ** head_pos
    part_scale = jnp.where(jnp.arange(3)[None, :] == 2, value_scale[:, None], 1.0)
    drawn = base * part_scale[None, :, :, None] * D ** (-0.5)
    return drawn.reshape(D, H * 3 * HEAD).astype(jnp.bfloat16)


def block_levels(key, extent, pieces, low, largest):
    def one(axis_at, shards_of):
        draws = jax.random.uniform(jax.random.fold_in(jax.random.fold_in(key, 6), axis_at), (shards_of,), jnp.float32, low / len(pieces), largest / len(pieces))
        return jnp.repeat(jnp.exp(draws), extent[axis_at] // shards_of).reshape((-1,) + (1,) * (len(extent) - axis_at - 1))

    gain = one(*pieces[0])
    for cut in pieces[1:]:
        gain = gain * one(*cut)
    return gain


def gaussian(stream_key, dims, spread, most, pieces=(), kind=jnp.bfloat16):
    result = spread * jax.random.normal(stream_key, dims, jnp.float32)
    if pieces:
        result = result * block_levels(stream_key, dims, pieces, -0.22, 0.18)
    return jnp.clip(result, -most, most).astype(kind)


def setup_inputs(seed: int = 0) -> dict:
    seeds = jax.random.split(jax.random.key(seed), 5)
    return {
        "tokens_t": gaussian(seeds[0], (D, TOKENS), 1.0, 6.0, ((0, 32), (1, 32))),
        "qkv_weight": draw_qkv_weight(jax.random.fold_in(seeds[4], 71), 0),
        "prior_state": gaussian(seeds[2], (H, HEAD, HEAD), (GROUP / 8), 192.0, ((0, 32),), jnp.float32),
        "norm_gain": jnp.clip(1.0 + 0.18 * jax.random.normal(seeds[3], (H * HEAD,), jnp.float32), 0.1, 1.9),
    }


EPSILON = 1e-06
PRECISE = lax.Precision.HIGHEST

def reference(tokens_t, qkv_weight, prior_state, norm_gain):
    features = tokens_t.T.astype(jnp.float32)
    stacked = qkv_weight.reshape(D, H, 3 * HEAD).transpose(1, 0, 2)
    causal = jnp.arange(GROUP)[:, None] >= jnp.arange(GROUP)[None, :]

    def one_head(operands):
        w_head, prior_kv = operands
        projected = jnp.dot(features, w_head.astype(jnp.float32), preferred_element_type=jnp.float32, precision=PRECISE)
        activated = lax.optimization_barrier(jax.nn.silu(projected).astype(jnp.bfloat16)).astype(jnp.float32)
        blocks = activated.reshape(N_CONTEXT, GROUP, 3, HEAD)
        queries = blocks[:, :, 0]
        key_rows = blocks[:, :, 1]
        value_rows = blocks[:, :, 2]
        states = jnp.einsum('ctd,cte->cde', key_rows, value_rows, precision=PRECISE)
        zero_state = jnp.zeros((1, HEAD, HEAD), jnp.float32)
        carried = prior_kv[None] + jnp.concatenate([zero_state, jnp.cumsum(states, axis=0)[:-1]], axis=0)
        scores = jnp.einsum('ctd,csd->cts', queries, key_rows, precision=PRECISE)
        scores = jnp.where(causal[None], scores, 0.0)
        scores = lax.optimization_barrier(scores.astype(jnp.bfloat16)).astype(jnp.float32)
        within = jnp.einsum('cts,csd->ctd', scores, value_rows, precision=PRECISE)
        across = jnp.einsum('ctd,cde->cte', queries, carried, precision=PRECISE)
        return (within + across).reshape(TOKENS, HEAD)
    attended = lax.map(one_head, (stacked, prior_state.astype(jnp.float32)))
    attended = attended.transpose(1, 0, 2).reshape(TOKENS, H * HEAD)
    mean_sq = lax.optimization_barrier(jnp.mean(attended * attended, axis=1, keepdims=True))
    return (attended * lax.rsqrt(mean_sq + EPSILON) * norm_gain[None, :]).astype(jnp.bfloat16)
```

```python
import functools

import jax
import jax.numpy as jnp
from jax import lax
from jax.experimental import pallas as pl
from jax.experimental.pallas import tpu as pltpu
from jax.sharding import PartitionSpec as P

HEAD = 128
EPSILON = 1e-06
CHUNKS = 4
X_CHIPS = 4
F32 = jnp.float32
BF16 = jnp.bfloat16
MESH = pl.DeviceIdType.MESH


def silu(u):
    return u / (1.0 + jnp.exp(-u))


def wait_bytes(ref, sem):
    pltpu.make_async_copy(ref, ref, sem).wait()


def kernel(
    nc, nx, nz, width,
    x_ref, w_ref, prior_ref, gain_ref, out_ref,
    xbuf, wbuf, prior, gain, acc, sbuf, gath, pref, carr, ssq,
    send, recv, local, send1, recv1, send2, recv2, send3, recv3,
):
    ny = nc // (2 * nx)
    half = nz // 2
    rows = xbuf.shape[1]
    piece = rows // CHUNKS
    heads = prior_ref.shape[0]
    c = lax.axis_index("context")
    z = lax.axis_index("tensor")
    neighbour = (lax.rem(z + 1, nz), lax.rem(z + nz - 1, nz))

    px, py, pk = c // (2 * ny), lax.rem(c // 2, ny), lax.rem(c, 2)
    offsets = [(dx, dy, dk) for dx in range(nx) for dy in range(ny) for dk in range(2)]
    offsets = sorted(offsets[1:], key=lambda o: -(min(o[0], nx - o[0]) + min(o[1], ny - o[1])))

    def peer(offset):
        dx, dy, dk = offset
        return (lax.rem(px + dx, nx) * ny + lax.rem(py + dy, ny)) * 2 + lax.rem(pk + dk, 2)

    own = pltpu.make_async_copy(x_ref, xbuf.at[z], local.at[0])
    weights = pltpu.make_async_copy(w_ref, wbuf, local.at[1])
    prior_in = pltpu.make_async_copy(prior_ref, prior, local.at[2])
    gain_in = pltpu.make_async_copy(gain_ref, gain, local.at[3])

    barrier = pltpu.get_barrier_semaphore()
    for d in range(2):
        pl.semaphore_signal(
            barrier, inc=1, device_id={"tensor": neighbour[d]}, device_id_type=MESH
        )
    for offset in offsets:
        pl.semaphore_signal(
            barrier, inc=1, device_id={"context": peer(offset)}, device_id_type=MESH
        )
    own.start()
    weights.start()
    prior_in.start()
    gain_in.start()
    pl.semaphore_wait(barrier, len(offsets) + 2)

    def source(d, s):
        return lax.rem(z + (nz - s if d == 0 else s), nz)

    def part(j):
        return pl.ds(j * piece, piece)

    def forward(d, s, j, src):
        at = source(d, s)
        pltpu.make_async_remote_copy(
            src_ref=src,
            dst_ref=xbuf.at[at, part(j)],
            send_sem=send.at[d, s, j],
            recv_sem=recv.at[d, s + 1, j],
            device_id={"tensor": neighbour[d]},
            device_id_type=MESH,
        ).start()

    def arrived(d, s, j):
        wait_bytes(xbuf.at[source(d, s), part(j)], recv.at[d, s, j])

    def project(at):
        return lax.dot_general(
            xbuf[at], wbuf[at], (((0,), (0,)), ((), ())), preferred_element_type=F32
        )

    for j in range(CHUNKS):
        for d in range(2):
            forward(d, 0, j, x_ref.at[part(j)])

    def relay(s, final):
        for j in range(CHUNKS):
            for d in range(2):
                arrived(d, s, j)
                if not final or (j < CHUNKS // 2) == (d == 0):
                    forward(d, s, j, xbuf.at[source(d, s), part(j)])

    relay(1, False)
    own.wait()
    weights.wait()
    acc[...] = project(z)

    @pl.loop(2, half - 1)
    def _(s):
        relay(s, False)
        acc[...] += project(source(0, s - 1)) + project(source(1, s - 1))

    relay(half - 1, True)
    for s in (half - 2, half - 1):
        acc[...] += project(source(0, s)) + project(source(1, s))
    for j in range(CHUNKS):
        arrived(0 if j < CHUNKS // 2 else 1, half, j)
    acc[...] += project(source(0, half))

    keys, values = [], []
    per = nc // heads
    for h in range(heads):
        base = h * 3 * HEAD
        keys.append(silu(acc[:, base + HEAD : base + 2 * HEAD]).astype(BF16))
        values.append(silu(acc[:, base + 2 * HEAD : base + 3 * HEAD]).astype(BF16))
        state = lax.dot_general(
            keys[h], values[h], (((0,), (0,)), ((), ())), preferred_element_type=F32
        )
        sbuf[h * per : (h + 1) * per] = state.reshape(per, HEAD // per, HEAD)

    def exchange(src, dst, send_sem, recv_sem):
        for offset in offsets:
            to = peer(offset)
            pltpu.make_async_remote_copy(
                src_ref=src.at[to],
                dst_ref=dst.at[c],
                send_sem=send_sem,
                recv_sem=recv_sem,
                device_id={"context": to},
                device_id_type=MESH,
            ).start()

    others = pl.ds(0, nc - 1)
    exchange(sbuf, gath, send1, recv1)
    gath[c] = sbuf[c]

    queries, within = [], []
    tokens = acc.shape[0]
    causal = lax.broadcasted_iota(jnp.int32, (tokens, tokens), 0) >= lax.broadcasted_iota(
        jnp.int32, (tokens, tokens), 1
    )
    for h in range(heads):
        base = h * 3 * HEAD
        queries.append(silu(acc[:, base : base + HEAD]).astype(BF16))
        scores = lax.dot_general(
            queries[h], keys[h], (((1,), (1,)), ((), ())), preferred_element_type=F32
        )
        scores = jnp.where(causal, scores, 0.0).astype(BF16)
        within.append(jnp.dot(scores, values[h], preferred_element_type=F32))

    wait_bytes(gath.at[others], recv1)
    running = jnp.zeros(gath.shape[1:], F32)
    for i in range(nc):
        pref[i] = running
        running = running + gath[i]
    exchange(pref, carr, send2, recv2)
    carr[c] = pref[c]
    prior_in.wait()
    gain_in.wait()
    wait_bytes(carr.at[others], recv2)

    attended = []
    for h in range(heads):
        carried = prior[h] + carr[h * per : (h + 1) * per].reshape(HEAD, HEAD)
        high = carried.astype(BF16)
        low = (carried - high.astype(F32)).astype(BF16)
        across = jnp.dot(queries[h], high, preferred_element_type=F32)
        across += jnp.dot(queries[h], low, preferred_element_type=F32)
        attended.append(within[h] + across)
    squares = attended[0] * attended[0]
    for h in range(1, heads):
        squares += attended[h] * attended[h]
    ssq[z] = jnp.sum(squares.T, axis=0, keepdims=True)

    def tell(to):
        pltpu.make_async_remote_copy(
            src_ref=ssq.at[z],
            dst_ref=ssq.at[z],
            send_sem=send3,
            recv_sem=recv3,
            device_id={"tensor": to},
            device_id_type=MESH,
        ).start()

    tell(source(1, half))

    @pl.loop(1, half)
    def _(i):
        tell(source(0, half - i))
        tell(source(1, half - i))

    peers = pl.ds(0, nz - 1)
    wait_bytes(ssq.at[peers], recv3)
    total = jnp.sum(ssq[...], axis=0)
    inverse = lax.rsqrt(total / width + EPSILON)
    column = jnp.broadcast_to(inverse, (HEAD, tokens)).T
    for h in range(heads):
        span = slice(h * HEAD, (h + 1) * HEAD)
        out_ref[:, span] = (attended[h] * column * gain[:, span]).astype(out_ref.dtype)

    wait_bytes(sbuf.at[others], send1)
    wait_bytes(pref.at[others], send2)
    wait_bytes(ssq.at[peers], send3)

    @pl.loop(0, half - 1)
    def _(s):
        for j in range(CHUNKS):
            for d in range(2):
                wait_bytes(xbuf.at[z, part(j)], send.at[d, s, j])

    for j in range(CHUNKS):
        wait_bytes(xbuf.at[z, part(j)], send.at[0 if j < CHUNKS // 2 else 1, half - 1, j])


def solution(mesh):
    nc, nz = mesh.shape["context"], mesh.shape["tensor"]
    nx = X_CHIPS if nc == 2 * X_CHIPS * X_CHIPS else 2

    def body(tokens_t, qkv_weight, prior_state, norm_gain):
        rows, tokens = tokens_t.shape
        heads = prior_state.shape[0]
        columns = qkv_weight.shape[1]
        tile = heads * HEAD // nc
        width = norm_gain.shape[0] * nz
        any_space = pl.BlockSpec(memory_space=pl.ANY)
        return pl.pallas_call(
            functools.partial(kernel, nc, nx, nz, width),
            out_shape=jax.ShapeDtypeStruct((tokens, heads * HEAD), BF16),
            in_specs=[any_space] * 4,
            out_specs=pl.BlockSpec(memory_space=pltpu.VMEM),
            scratch_shapes=[
                pltpu.VMEM((nz, rows, tokens), BF16),
                pltpu.VMEM((nz, rows, columns), BF16),
                pltpu.VMEM((heads, HEAD, HEAD), F32),
                pltpu.VMEM((1, heads * HEAD), F32),
                pltpu.VMEM((tokens, columns), F32),
                pltpu.VMEM((nc, tile, HEAD), F32),
                pltpu.VMEM((nc, tile, HEAD), F32),
                pltpu.VMEM((nc, tile, HEAD), F32),
                pltpu.VMEM((nc, tile, HEAD), F32),
                pltpu.VMEM((nz, 1, tokens), F32),
                pltpu.SemaphoreType.DMA((2, nz // 2, CHUNKS)),
                pltpu.SemaphoreType.DMA((2, nz // 2 + 1, CHUNKS)),
                pltpu.SemaphoreType.DMA((4,)),
            ]
            + [pltpu.SemaphoreType.DMA] * 6,
            compiler_params=pltpu.CompilerParams(
                collective_id=0, has_side_effects=True, vmem_limit_bytes=48 << 20
            ),
        )(
            tokens_t,
            qkv_weight.reshape(nz, rows, columns),
            prior_state,
            norm_gain.reshape(1, -1),
        )

    in_specs = (P("tensor", "context"), P(None, "tensor"), P("tensor", None, None), P("tensor"))
    out_specs = P("context", "tensor")
    return jax.shard_map(body, mesh=mesh, in_specs=in_specs, out_specs=out_specs, check_vma=False)
```

```python
import functools

import jax
import jax.numpy as jnp
from jax import lax
from jax.experimental import pallas as pl
from jax.experimental.pallas import tpu as pltpu
from jax.sharding import PartitionSpec as P

HEAD = 128
EPSILON = 1e-06
CHUNKS = 4
X_CHIPS = 4
F32 = jnp.float32
BF16 = jnp.bfloat16
MESH = pl.DeviceIdType.MESH


def silu(u):
    return u / (1.0 + jnp.exp(-u))


def wait_bytes(ref, sem):
    pltpu.make_async_copy(ref, ref, sem).wait()


def kernel(
    nc, nx, nz, width,
    x_ref, w_ref, prior_ref, gain_ref, out_ref,
    xbuf, wbuf, prior, gain, acc, sbuf, gath, pref, carr, ssq,
    send, recv, local, send1, recv1, send2, recv2, send3, recv3, entered,
):
    ny = nc // (2 * nx)
    half = nz // 2
    rows = xbuf.shape[1]
    piece = rows // CHUNKS
    heads = prior_ref.shape[0]
    c = lax.axis_index("context")
    z = lax.axis_index("tensor")
    neighbour = (lax.rem(z + 1, nz), lax.rem(z + nz - 1, nz))

    px, py, pk = c // (2 * ny), lax.rem(c // 2, ny), lax.rem(c, 2)

    def at_chip(x, y, k):
        return (x * ny + y) * 2 + k

    sibling = at_chip(px, py, 1 - pk)
    along_y = [at_chip(px, lax.rem(py + d, ny), pk) for d in (1, ny - 1)]
    along_x = [at_chip(lax.rem(px + d, nx), py, pk) for d in (1, nx - 1)]

    def signal(sem, to):
        pl.semaphore_signal(sem, inc=1, device_id={"context": to}, device_id_type=MESH)

    own = pltpu.make_async_copy(x_ref, xbuf.at[z], local.at[0])
    weights = pltpu.make_async_copy(w_ref, wbuf, local.at[1])
    prior_in = pltpu.make_async_copy(prior_ref, prior, local.at[2])
    gain_in = pltpu.make_async_copy(gain_ref, gain, local.at[3])

    barrier = pltpu.get_barrier_semaphore()
    for d in range(2):
        pl.semaphore_signal(
            barrier, inc=1, device_id={"tensor": neighbour[d]}, device_id_type=MESH
        )
    for to in [sibling] + along_y + along_x:
        signal(barrier, to)
    own.start()
    weights.start()
    prior_in.start()
    gain_in.start()
    pl.semaphore_wait(barrier, 7)

    def source(d, s):
        return lax.rem(z + (nz - s if d == 0 else s), nz)

    def part(j):
        return pl.ds(j * piece, piece)

    def forward(d, s, j, src):
        at = source(d, s)
        pltpu.make_async_remote_copy(
            src_ref=src,
            dst_ref=xbuf.at[at, part(j)],
            send_sem=send.at[d, s, j],
            recv_sem=recv.at[d, s + 1, j],
            device_id={"tensor": neighbour[d]},
            device_id_type=MESH,
        ).start()

    def arrived(d, s, j):
        wait_bytes(xbuf.at[source(d, s), part(j)], recv.at[d, s, j])

    def project(at):
        return lax.dot_general(
            xbuf[at], wbuf[at], (((0,), (0,)), ((), ())), preferred_element_type=F32
        )

    for j in range(CHUNKS):
        for d in range(2):
            forward(d, 0, j, x_ref.at[part(j)])

    def relay(s, final):
        for j in range(CHUNKS):
            for d in range(2):
                arrived(d, s, j)
                if not final or (j < CHUNKS // 2) == (d == 0):
                    forward(d, s, j, xbuf.at[source(d, s), part(j)])

    for to in along_y:
        signal(entered.at[0], to)
    relay(1, False)
    pl.semaphore_wait(entered.at[0], 2)
    for to in along_x:
        signal(entered.at[1], to)
    relay(2, False)
    own.wait()
    weights.wait()
    acc[...] = project(z) + project(source(0, 1)) + project(source(1, 1))

    @pl.loop(3, half - 1)
    def _(s):
        relay(s, False)
        acc[...] += project(source(0, s - 1)) + project(source(1, s - 1))

    pl.semaphore_wait(entered.at[1], 2)
    for to in along_x:
        signal(entered.at[2], to)
    relay(half - 1, True)
    for s in (half - 2, half - 1):
        acc[...] += project(source(0, s)) + project(source(1, s))
    pl.semaphore_wait(entered.at[2], 2)
    signal(entered.at[3], sibling)
    last = source(0, half)
    for j in range(CHUNKS):
        arrived(0 if j < CHUNKS // 2 else 1, half, j)

    def activated(begin, count):
        span = pl.ds(begin * HEAD, count * HEAD)
        u = acc[:, span] + lax.dot_general(
            xbuf[last], wbuf[last, :, span], (((0,), (0,)), ((), ())), preferred_element_type=F32
        )
        return silu(u).astype(BF16)

    def exchange(h, src, dst, send_sem, recv_sem):
        for dy in sorted(range(ny), key=lambda d: -min(d, ny - d)):
            for x in range(h * nx // heads, (h + 1) * nx // heads):
                for dk in (1, 0):
                    to = at_chip(x, lax.rem(py + dy, ny), pk if dk == 0 else 1 - pk)
                    copy = pltpu.make_async_remote_copy(
                        src_ref=src.at[to],
                        dst_ref=dst.at[c],
                        send_sem=send_sem,
                        recv_sem=recv_sem,
                        device_id={"context": to},
                        device_id_type=MESH,
                    )
                    if dy or dk:
                        copy.start()
                    else:
                        pl.when(px != x)(copy.start)

    others = pl.ds(0, nc - 1)
    keys, values = [], []
    per = nc // heads
    for h in range(heads):
        pair = activated(3 * h + 1, 2)
        keys.append(pair[:, :HEAD])
        values.append(pair[:, HEAD:])
        state = lax.dot_general(
            keys[h], values[h], (((0,), (0,)), ((), ())), preferred_element_type=F32
        )
        sbuf[h * per : (h + 1) * per] = state.reshape(per, HEAD // per, HEAD)
        if h == 0:
            pl.semaphore_wait(entered.at[3], 1)
        exchange(h, sbuf, gath, send1, recv1)
    gath[c] = sbuf[c]

    queries, within = [], []
    tokens = acc.shape[0]
    causal = lax.broadcasted_iota(jnp.int32, (tokens, tokens), 0) >= lax.broadcasted_iota(
        jnp.int32, (tokens, tokens), 1
    )
    for h in range(heads):
        queries.append(activated(3 * h, 1))
        scores = lax.dot_general(
            queries[h], keys[h], (((1,), (1,)), ((), ())), preferred_element_type=F32
        )
        scores = jnp.where(causal, scores, 0.0).astype(BF16)
        within.append(jnp.dot(scores, values[h], preferred_element_type=F32))

    wait_bytes(gath.at[others], recv1)
    running = jnp.zeros(gath.shape[1:], F32)
    for i in range(nc):
        pref[i] = running
        running = running + gath[i]
    for h in range(heads):
        exchange(h, pref, carr, send2, recv2)
    carr[c] = pref[c]
    prior_in.wait()
    gain_in.wait()
    wait_bytes(carr.at[others], recv2)

    attended = []
    for h in range(heads):
        carried = prior[h] + carr[h * per : (h + 1) * per].reshape(HEAD, HEAD)
        high = carried.astype(BF16)
        low = (carried - high.astype(F32)).astype(BF16)
        across = jnp.dot(queries[h], high, preferred_element_type=F32)
        across += jnp.dot(queries[h], low, preferred_element_type=F32)
        attended.append(within[h] + across)
    squares = attended[0] * attended[0]
    for h in range(1, heads):
        squares += attended[h] * attended[h]
    ssq[z] = jnp.sum(squares.T, axis=0, keepdims=True)

    def tell(to):
        pltpu.make_async_remote_copy(
            src_ref=ssq.at[z],
            dst_ref=ssq.at[z],
            send_sem=send3,
            recv_sem=recv3,
            device_id={"tensor": to},
            device_id_type=MESH,
        ).start()

    tell(source(1, half))

    @pl.loop(1, half)
    def _(i):
        tell(source(0, half - i))
        tell(source(1, half - i))

    peers = pl.ds(0, nz - 1)
    wait_bytes(ssq.at[peers], recv3)
    total = jnp.sum(ssq[...], axis=0)
    inverse = lax.rsqrt(total / width + EPSILON)
    column = jnp.broadcast_to(inverse, (HEAD, tokens)).T
    for h in range(heads):
        span = slice(h * HEAD, (h + 1) * HEAD)
        out_ref[:, span] = (attended[h] * column * gain[:, span]).astype(out_ref.dtype)

    wait_bytes(sbuf.at[others], send1)
    wait_bytes(pref.at[others], send2)
    wait_bytes(ssq.at[peers], send3)

    @pl.loop(0, half - 1)
    def _(s):
        for j in range(CHUNKS):
            for d in range(2):
                wait_bytes(xbuf.at[z, part(j)], send.at[d, s, j])

    for j in range(CHUNKS):
        wait_bytes(xbuf.at[z, part(j)], send.at[0 if j < CHUNKS // 2 else 1, half - 1, j])


def solution(mesh):
    nc, nz = mesh.shape["context"], mesh.shape["tensor"]
    nx = X_CHIPS if nc == 2 * X_CHIPS * X_CHIPS else 2

    def body(tokens_t, qkv_weight, prior_state, norm_gain):
        rows, tokens = tokens_t.shape
        heads = prior_state.shape[0]
        columns = qkv_weight.shape[1]
        tile = heads * HEAD // nc
        width = norm_gain.shape[0] * nz
        any_space = pl.BlockSpec(memory_space=pl.ANY)
        return pl.pallas_call(
            functools.partial(kernel, nc, nx, nz, width),
            out_shape=jax.ShapeDtypeStruct((tokens, heads * HEAD), BF16),
            in_specs=[any_space] * 4,
            out_specs=pl.BlockSpec(memory_space=pltpu.VMEM),
            scratch_shapes=[
                pltpu.VMEM((nz, rows, tokens), BF16),
                pltpu.VMEM((nz, rows, columns), BF16),
                pltpu.VMEM((heads, HEAD, HEAD), F32),
                pltpu.VMEM((1, heads * HEAD), F32),
                pltpu.VMEM((tokens, columns), F32),
                pltpu.VMEM((nc, tile, HEAD), F32),
                pltpu.VMEM((nc, tile, HEAD), F32),
                pltpu.VMEM((nc, tile, HEAD), F32),
                pltpu.VMEM((nc, tile, HEAD), F32),
                pltpu.VMEM((nz, 1, tokens), F32),
                pltpu.SemaphoreType.DMA((2, nz // 2, CHUNKS)),
                pltpu.SemaphoreType.DMA((2, nz // 2 + 1, CHUNKS)),
                pltpu.SemaphoreType.DMA((4,)),
            ]
            + [pltpu.SemaphoreType.DMA] * 6
            + [pltpu.SemaphoreType.REGULAR((4,))],
            compiler_params=pltpu.CompilerParams(
                collective_id=0, has_side_effects=True, vmem_limit_bytes=60 * 1024 * 1024
            ),
        )(
            tokens_t,
            qkv_weight.reshape(nz, rows, columns),
            prior_state,
            norm_gain.reshape(1, -1),
        )

    in_specs = (P("tensor", "context"), P(None, "tensor"), P("tensor", None, None), P("tensor"))
    out_specs = P("context", "tensor")
    return jax.shard_map(body, mesh=mesh, in_specs=in_specs, out_specs=out_specs, check_vma=False)
```

```python
import functools

import jax
import jax.numpy as jnp
from jax import lax
from jax.experimental import pallas as pl
from jax.experimental.pallas import tpu as pltpu
from jax.sharding import PartitionSpec as P

HEAD = 128
EPSILON = 1e-06
CHUNKS = 4
X_CHIPS = 4
F32 = jnp.float32
BF16 = jnp.bfloat16
MESH = pl.DeviceIdType.MESH


def silu(u):
    return u / (1.0 + jnp.exp(-u))


def wait_bytes(ref, sem):
    pltpu.make_async_copy(ref, ref, sem).wait()


def kernel(
    nc, nx, nz, width,
    x_ref, w_ref, prior_ref, gain_ref, out_ref,
    xbuf, wbuf, prior, gain, acc, sbuf, gath, pref, carr, ssq,
    send, recv, local, send1, recv1, send2, recv2, send3, recv3, entered,
):
    ny = nc // (2 * nx)
    half = nz // 2
    rows = xbuf.shape[1]
    piece = rows // CHUNKS
    heads = prior_ref.shape[0]
    c = lax.axis_index("context")
    z = lax.axis_index("tensor")

    px, py, pk = c // (2 * ny), lax.rem(c // 2, ny), lax.rem(c, 2)

    def at_chip(x, y, k):
        return (x * ny + y) * 2 + k

    sibling = at_chip(px, py, 1 - pk)
    along_y = [at_chip(px, lax.rem(py + d, ny), pk) for d in (1, ny - 1)]
    along_x = [at_chip(lax.rem(px + d, nx), py, pk) for d in (1, nx - 1)]

    def signal(sem, to):
        pl.semaphore_signal(sem, inc=1, device_id={"context": to}, device_id_type=MESH)

    own = pltpu.make_async_copy(x_ref, xbuf.at[z], local.at[0])
    weights = pltpu.make_async_copy(w_ref, wbuf, local.at[1])
    prior_in = pltpu.make_async_copy(prior_ref, prior, local.at[2])
    gain_in = pltpu.make_async_copy(gain_ref, gain, local.at[3])

    barrier = pltpu.get_barrier_semaphore()
    for away in (1, 2, nz - 2, nz - 1):
        pl.semaphore_signal(
            barrier, inc=1, device_id={"tensor": lax.rem(z + away, nz)}, device_id_type=MESH
        )
    for to in [sibling] + along_y + along_x:
        signal(barrier, to)
    own.start()
    weights.start()
    prior_in.start()
    gain_in.start()
    pl.semaphore_wait(barrier, 9)

    def source(d, s):
        return lax.rem(z + (nz - s if d == 0 else s), nz)

    def part(j):
        return pl.ds(j * piece, piece)

    def forward(d, s, a, j, src):
        at = source(d, s)
        pltpu.make_async_remote_copy(
            src_ref=src,
            dst_ref=xbuf.at[at, part(j)],
            send_sem=send.at[d, a - 1, j],
            recv_sem=recv.at[d, a, j],
            device_id={"tensor": source(1 - d, a - s)},
            device_id_type=MESH,
        ).start()

    def arrived(d, s, j):
        wait_bytes(xbuf.at[source(d, s), part(j)], recv.at[d, s, j])

    def project(at):
        return lax.dot_general(
            xbuf[at], wbuf[at], (((0,), (0,)), ((), ())), preferred_element_type=F32
        )

    both = [(d, j) for j in range(CHUNKS) for d in range(2)]
    stops, ready = {}, {}
    for d, j in both:
        end = half if (j < CHUNKS // 2) == (d == 0) else half - 1
        stops[d, j] = [0]
        while stops[d, j][-1] < end:
            t, at = len(stops[d, j]) - 1, stops[d, j][-1]
            step = 2 if t % CHUNKS == j and at + 2 <= end else 1
            for between in range(1, step + 1):
                ready[d, at + between, j] = t + 1
            stops[d, j].append(at + step)
    hops = max(len(stop) for stop in stops.values()) - 1

    pending = [(d, a) for a in range(half) for d in range(2 if a else 1)]
    waited = set()

    def need(d, a, j):
        if (d, a, j) not in waited:
            waited.add((d, a, j))
            arrived(d, a, j)

    def gathered(d, a):
        for j in range(CHUNKS if a else 0):
            need(d, a, j)

    def project_one(t):
        if pending:
            d, a = pending[0]
            if max([ready[d, a, j] for j in range(CHUNKS)] if a else [1]) <= t:
                pending.pop(0)
                gathered(d, a)
                if a == 0:
                    own.wait()
                    weights.wait()
                    acc[...] = project(z)
                else:
                    acc[...] += project(source(d, a))

    def greet(t):
        if t == 0:
            for to in along_y:
                signal(entered.at[0], to)
        elif t == 2:
            pl.semaphore_wait(entered.at[0], 2)
            for to in along_x:
                signal(entered.at[1], to)
        elif t == hops - 2:
            pl.semaphore_wait(entered.at[1], 2)
            for to in along_x:
                signal(entered.at[2], to)
        elif t == hops - 1:
            pl.semaphore_wait(entered.at[2], 2)
            signal(entered.at[3], sibling)

    for t in range(hops):
        for group in range(2):
            now = both[group * CHUNKS : (group + 1) * CHUNKS]
            now = [(d, j) for d, j in now if t + 1 < len(stops[d, j])]
            for d, j in now:
                at, to = stops[d, j][t], stops[d, j][t + 1]
                if t:
                    need(d, at, j)
                block = xbuf.at[source(d, at), part(j)] if t else x_ref.at[part(j)]
                forward(d, at, to, j, block)
            for d, j in now:
                at, to = stops[d, j][t], stops[d, j][t + 1]
                if to - at == 2:
                    block = xbuf.at[source(d, at), part(j)] if t else x_ref.at[part(j)]
                    forward(d, at, at + 1, j, block)
            if t >= 3:
                project_one(t - 1)
        greet(t)
    while pending:
        project_one(hops)
    last = source(0, half)
    for d, j in both:
        if stops[d, j][-1] == half:
            need(d, half, j)

    def activated(begin, count):
        span = pl.ds(begin * HEAD, count * HEAD)
        u = acc[:, span] + lax.dot_general(
            xbuf[last], wbuf[last, :, span], (((0,), (0,)), ((), ())), preferred_element_type=F32
        )
        return silu(u).astype(BF16)

    def exchange(h, src, dst, send_sem, recv_sem):
        for dy in sorted(range(ny), key=lambda d: -min(d, ny - d)):
            for x in range(h * nx // heads, (h + 1) * nx // heads):
                for dk in (1, 0):
                    to = at_chip(x, lax.rem(py + dy, ny), pk if dk == 0 else 1 - pk)
                    copy = pltpu.make_async_remote_copy(
                        src_ref=src.at[to],
                        dst_ref=dst.at[c],
                        send_sem=send_sem,
                        recv_sem=recv_sem,
                        device_id={"context": to},
                        device_id_type=MESH,
                    )
                    if dy or dk:
                        copy.start()
                    else:
                        pl.when(px != x)(copy.start)

    others = pl.ds(0, nc - 1)
    keys, values = [], []
    per = nc // heads
    for h in range(heads):
        pair = activated(3 * h + 1, 2)
        keys.append(pair[:, :HEAD])
        values.append(pair[:, HEAD:])
        state = lax.dot_general(
            keys[h], values[h], (((0,), (0,)), ((), ())), preferred_element_type=F32
        )
        sbuf[h * per : (h + 1) * per] = state.reshape(per, HEAD // per, HEAD)
        if h == 0:
            pl.semaphore_wait(entered.at[3], 1)
        exchange(h, sbuf, gath, send1, recv1)
    gath[c] = sbuf[c]

    queries, within = [], []
    tokens = acc.shape[0]
    causal = lax.broadcasted_iota(jnp.int32, (tokens, tokens), 0) >= lax.broadcasted_iota(
        jnp.int32, (tokens, tokens), 1
    )
    for h in range(heads):
        queries.append(activated(3 * h, 1))
        scores = lax.dot_general(
            queries[h], keys[h], (((1,), (1,)), ((), ())), preferred_element_type=F32
        )
        scores = jnp.where(causal, scores, 0.0).astype(BF16)
        within.append(jnp.dot(scores, values[h], preferred_element_type=F32))

    wait_bytes(gath.at[others], recv1)
    running = jnp.zeros(gath.shape[1:], F32)
    for i in range(nc):
        pref[i] = running
        running = running + gath[i]
    for h in range(heads):
        exchange(h, pref, carr, send2, recv2)
    carr[c] = pref[c]
    prior_in.wait()
    gain_in.wait()
    wait_bytes(carr.at[others], recv2)

    attended = []
    for h in range(heads):
        carried = prior[h] + carr[h * per : (h + 1) * per].reshape(HEAD, HEAD)
        high = carried.astype(BF16)
        low = (carried - high.astype(F32)).astype(BF16)
        across = jnp.dot(queries[h], high, preferred_element_type=F32)
        across += jnp.dot(queries[h], low, preferred_element_type=F32)
        attended.append(within[h] + across)
    squares = attended[0] * attended[0]
    for h in range(1, heads):
        squares += attended[h] * attended[h]
    ssq[z] = jnp.sum(squares.T, axis=0, keepdims=True)

    def tell(to):
        pltpu.make_async_remote_copy(
            src_ref=ssq.at[z],
            dst_ref=ssq.at[z],
            send_sem=send3,
            recv_sem=recv3,
            device_id={"tensor": to},
            device_id_type=MESH,
        ).start()

    tell(source(1, half))

    @pl.loop(1, half)
    def _(i):
        tell(source(0, half - i))
        tell(source(1, half - i))

    peers = pl.ds(0, nz - 1)
    wait_bytes(ssq.at[peers], recv3)
    total = jnp.sum(ssq[...], axis=0)
    inverse = lax.rsqrt(total / width + EPSILON)
    column = jnp.broadcast_to(inverse, (HEAD, tokens)).T
    for h in range(heads):
        span = slice(h * HEAD, (h + 1) * HEAD)
        out_ref[:, span] = (attended[h] * column * gain[:, span]).astype(out_ref.dtype)

    wait_bytes(sbuf.at[others], send1)
    wait_bytes(pref.at[others], send2)
    wait_bytes(ssq.at[peers], send3)

    @pl.loop(0, half - 1)
    def _(s):
        for j in range(CHUNKS):
            for d in range(2):
                wait_bytes(xbuf.at[z, part(j)], send.at[d, s, j])

    for j in range(CHUNKS):
        wait_bytes(xbuf.at[z, part(j)], send.at[0 if j < CHUNKS // 2 else 1, half - 1, j])


def solution(mesh):
    nc, nz = mesh.shape["context"], mesh.shape["tensor"]
    nx = X_CHIPS if nc == 2 * X_CHIPS * X_CHIPS else 2

    def body(tokens_t, qkv_weight, prior_state, norm_gain):
        rows, tokens = tokens_t.shape
        heads = prior_state.shape[0]
        columns = qkv_weight.shape[1]
        tile = heads * HEAD // nc
        width = norm_gain.shape[0] * nz
        any_space = pl.BlockSpec(memory_space=pl.ANY)
        return pl.pallas_call(
            functools.partial(kernel, nc, nx, nz, width),
            out_shape=jax.ShapeDtypeStruct((tokens, heads * HEAD), BF16),
            in_specs=[any_space] * 4,
            out_specs=pl.BlockSpec(memory_space=pltpu.VMEM),
            scratch_shapes=[
                pltpu.VMEM((nz, rows, tokens), BF16),
                pltpu.VMEM((nz, rows, columns), BF16),
                pltpu.VMEM((heads, HEAD, HEAD), F32),
                pltpu.VMEM((1, heads * HEAD), F32),
                pltpu.VMEM((tokens, columns), F32),
                pltpu.VMEM((nc, tile, HEAD), F32),
                pltpu.VMEM((nc, tile, HEAD), F32),
                pltpu.VMEM((nc, tile, HEAD), F32),
                pltpu.VMEM((nc, tile, HEAD), F32),
                pltpu.VMEM((nz, 1, tokens), F32),
                pltpu.SemaphoreType.DMA((2, nz // 2, CHUNKS)),
                pltpu.SemaphoreType.DMA((2, nz // 2 + 1, CHUNKS)),
                pltpu.SemaphoreType.DMA((4,)),
            ]
            + [pltpu.SemaphoreType.DMA] * 6
            + [pltpu.SemaphoreType.REGULAR((4,))],
            compiler_params=pltpu.CompilerParams(
                collective_id=0, has_side_effects=True, vmem_limit_bytes=60 * 1024 * 1024
            ),
        )(
            tokens_t,
            qkv_weight.reshape(nz, rows, columns),
            prior_state,
            norm_gain.reshape(1, -1),
        )

    in_specs = (P("tensor", "context"), P(None, "tensor"), P("tensor", None, None), P("tensor"))
    out_specs = P("context", "tensor")
    return jax.shard_map(body, mesh=mesh, in_specs=in_specs, out_specs=out_specs, check_vma=False)
```

```python
import functools

import jax
import jax.numpy as jnp
from jax import lax
from jax.experimental import pallas as pl
from jax.experimental.pallas import tpu as pltpu
from jax.sharding import PartitionSpec as P

HEAD = 128
EPSILON = 1e-06
CHUNKS = 4
X_CHIPS = 4
F32 = jnp.float32
BF16 = jnp.bfloat16
MESH = pl.DeviceIdType.MESH


def silu(u):
    return u / (1.0 + jnp.exp(-u))


def wait_bytes(ref, sem):
    pltpu.make_async_copy(ref, ref, sem).wait()


def kernel(
    nc, nx, nz, width,
    x_ref, w_ref, prior_ref, gain_ref, out_ref,
    xbuf, wbuf, prior, gain, acc, sbuf, gath, pref, carr, ssq,
    send, recv, local, send1, recv1, send2, recv2, send3, recv3, entered,
):
    ny = nc // (2 * nx)
    half = nz // 2
    rows = xbuf.shape[1]
    piece = rows // CHUNKS
    heads = prior_ref.shape[0]
    c = lax.axis_index("context")
    z = lax.axis_index("tensor")

    px, py, pk = c // (2 * ny), lax.rem(c // 2, ny), lax.rem(c, 2)

    def at_chip(x, y, k):
        return (x * ny + y) * 2 + k

    sibling = at_chip(px, py, 1 - pk)
    along_y = [at_chip(px, lax.rem(py + d, ny), pk) for d in (1, ny - 1)]
    along_x = [at_chip(lax.rem(px + d, nx), py, pk) for d in (1, nx - 1)]

    def signal(sem, to):
        pl.semaphore_signal(sem, inc=1, device_id={"context": to}, device_id_type=MESH)

    own = pltpu.make_async_copy(x_ref, xbuf.at[z], local.at[0])
    weights = pltpu.make_async_copy(w_ref, wbuf, local.at[1])
    prior_in = pltpu.make_async_copy(prior_ref, prior, local.at[2])
    gain_in = pltpu.make_async_copy(gain_ref, gain, local.at[3])

    barrier = pltpu.get_barrier_semaphore()
    for away in (1, 2, nz - 2, nz - 1):
        pl.semaphore_signal(
            barrier, inc=1, device_id={"tensor": lax.rem(z + away, nz)}, device_id_type=MESH
        )
    for to in [sibling] + along_y + along_x:
        signal(barrier, to)
    own.start()
    weights.start()
    prior_in.start()
    gain_in.start()
    pl.semaphore_wait(barrier, 9)

    def source(d, s):
        return lax.rem(z + (nz - s if d == 0 else s), nz)

    def part(j):
        return pl.ds(j * piece, piece)

    def forward(d, s, a, j, src):
        at = source(d, s)
        pltpu.make_async_remote_copy(
            src_ref=src,
            dst_ref=xbuf.at[at, part(j)],
            send_sem=send.at[d, a - 1, j],
            recv_sem=recv.at[d, a, j],
            device_id={"tensor": source(1 - d, a - s)},
            device_id_type=MESH,
        ).start()

    def arrived(d, s, j):
        wait_bytes(xbuf.at[source(d, s), part(j)], recv.at[d, s, j])

    def project(at):
        return lax.dot_general(
            xbuf[at], wbuf[at], (((0,), (0,)), ((), ())), preferred_element_type=F32
        )

    both = [(d, j) for j in range(CHUNKS) for d in range(2)]
    stops, ready = {}, {}
    for d, j in both:
        end = half if (j < CHUNKS // 2) == (d == 0) else half - 1
        stops[d, j] = [0]
        while stops[d, j][-1] < end:
            t, at = len(stops[d, j]) - 1, stops[d, j][-1]
            step = 2 if t % CHUNKS == j and at + 2 <= end else 1
            for between in range(1, step + 1):
                ready[d, at + between, j] = t + 1
            stops[d, j].append(at + step)
    hops = max(len(stop) for stop in stops.values()) - 1

    pending = [(d, a) for a in range(half) for d in range(2 if a else 1)]
    waited = set()

    def need(d, a, j):
        if (d, a, j) not in waited:
            waited.add((d, a, j))
            arrived(d, a, j)

    def gathered(d, a):
        for j in range(CHUNKS if a else 0):
            need(d, a, j)

    def project_one(t):
        if pending:
            d, a = pending[0]
            if max([ready[d, a, j] for j in range(CHUNKS)] if a else [1]) <= t:
                pending.pop(0)
                gathered(d, a)
                if a == 0:
                    own.wait()
                    weights.wait()
                    acc[...] = project(z)
                else:
                    acc[...] += project(source(d, a))

    def greet(t):
        if t == 0:
            for to in along_y:
                signal(entered.at[0], to)
        elif t == 2:
            pl.semaphore_wait(entered.at[0], 2)
            for to in along_x:
                signal(entered.at[1], to)
        elif t == hops - 2:
            pl.semaphore_wait(entered.at[1], 2)
            for to in along_x:
                signal(entered.at[2], to)
        elif t == hops - 1:
            pl.semaphore_wait(entered.at[2], 2)
            signal(entered.at[3], sibling)

    for t in range(hops):
        for group in range(2):
            now = both[group * CHUNKS : (group + 1) * CHUNKS]
            now = [(d, j) for d, j in now if t + 1 < len(stops[d, j])]
            for d, j in now:
                at, to = stops[d, j][t], stops[d, j][t + 1]
                if t:
                    need(d, at, j)
                block = xbuf.at[source(d, at), part(j)] if t else x_ref.at[part(j)]
                forward(d, at, to, j, block)
            for d, j in now:
                at, to = stops[d, j][t], stops[d, j][t + 1]
                if to - at == 2:
                    block = xbuf.at[source(d, at), part(j)] if t else x_ref.at[part(j)]
                    forward(d, at, at + 1, j, block)
            for _ in range(group + 1 if t >= 2 else 0):
                project_one(t - 1)
        greet(t)
    while pending:
        project_one(hops)
    last = source(0, half)
    for d, j in both:
        if stops[d, j][-1] == half:
            need(d, half, j)

    def activated(begin, count):
        span = pl.ds(begin * HEAD, count * HEAD)
        u = acc[:, span] + lax.dot_general(
            xbuf[last], wbuf[last, :, span], (((0,), (0,)), ((), ())), preferred_element_type=F32
        )
        return silu(u).astype(BF16)

    def exchange(h, src, dst, send_sem, recv_sem):
        for dy in sorted(range(ny), key=lambda d: -min(d, ny - d)):
            for x in range(h * nx // heads, (h + 1) * nx // heads):
                for dk in (1, 0):
                    to = at_chip(x, lax.rem(py + dy, ny), pk if dk == 0 else 1 - pk)
                    copy = pltpu.make_async_remote_copy(
                        src_ref=src.at[to],
                        dst_ref=dst.at[c],
                        send_sem=send_sem,
                        recv_sem=recv_sem,
                        device_id={"context": to},
                        device_id_type=MESH,
                    )
                    if dy or dk:
                        copy.start()
                    else:
                        pl.when(px != x)(copy.start)

    others = pl.ds(0, nc - 1)
    keys, values = [], []
    per = nc // heads
    for h in range(heads):
        pair = activated(3 * h + 1, 2)
        keys.append(pair[:, :HEAD])
        values.append(pair[:, HEAD:])
        state = lax.dot_general(
            keys[h], values[h], (((0,), (0,)), ((), ())), preferred_element_type=F32
        )
        sbuf[h * per : (h + 1) * per] = state.reshape(per, HEAD // per, HEAD)
        if h == 0:
            pl.semaphore_wait(entered.at[3], 1)
        exchange(h, sbuf, gath, send1, recv1)
    gath[c] = sbuf[c]

    queries, within = [], []
    tokens = acc.shape[0]
    causal = lax.broadcasted_iota(jnp.int32, (tokens, tokens), 0) >= lax.broadcasted_iota(
        jnp.int32, (tokens, tokens), 1
    )
    for h in range(heads):
        queries.append(activated(3 * h, 1))
        scores = lax.dot_general(
            queries[h], keys[h], (((1,), (1,)), ((), ())), preferred_element_type=F32
        )
        scores = jnp.where(causal, scores, 0.0).astype(BF16)
        within.append(jnp.dot(scores, values[h], preferred_element_type=F32))

    wait_bytes(gath.at[others], recv1)
    running = jnp.zeros(gath.shape[1:], F32)
    for i in range(nc):
        pref[i] = running
        running = running + gath[i]
    for h in range(heads):
        exchange(h, pref, carr, send2, recv2)
    carr[c] = pref[c]
    prior_in.wait()
    gain_in.wait()
    wait_bytes(carr.at[others], recv2)

    attended = []
    for h in range(heads):
        carried = prior[h] + carr[h * per : (h + 1) * per].reshape(HEAD, HEAD)
        high = carried.astype(BF16)
        low = (carried - high.astype(F32)).astype(BF16)
        across = jnp.dot(queries[h], high, preferred_element_type=F32)
        across += jnp.dot(queries[h], low, preferred_element_type=F32)
        attended.append(within[h] + across)
    squares = attended[0] * attended[0]
    for h in range(1, heads):
        squares += attended[h] * attended[h]
    ssq[z] = jnp.sum(squares.T, axis=0, keepdims=True)

    def tell(to):
        pltpu.make_async_remote_copy(
            src_ref=ssq.at[z],
            dst_ref=ssq.at[z],
            send_sem=send3,
            recv_sem=recv3,
            device_id={"tensor": to},
            device_id_type=MESH,
        ).start()

    tell(source(1, half))

    @pl.loop(1, half)
    def _(i):
        tell(source(0, half - i))
        tell(source(1, half - i))

    peers = pl.ds(0, nz - 1)
    wait_bytes(ssq.at[peers], recv3)
    total = jnp.sum(ssq[...], axis=0)
    inverse = lax.rsqrt(total / width + EPSILON)
    column = jnp.broadcast_to(inverse, (HEAD, tokens)).T
    for h in range(heads):
        span = slice(h * HEAD, (h + 1) * HEAD)
        out_ref[:, span] = (attended[h] * column * gain[:, span]).astype(out_ref.dtype)

    wait_bytes(sbuf.at[others], send1)
    wait_bytes(pref.at[others], send2)
    wait_bytes(ssq.at[peers], send3)

    @pl.loop(0, half - 1)
    def _(s):
        for j in range(CHUNKS):
            for d in range(2):
                wait_bytes(xbuf.at[z, part(j)], send.at[d, s, j])

    for j in range(CHUNKS):
        wait_bytes(xbuf.at[z, part(j)], send.at[0 if j < CHUNKS // 2 else 1, half - 1, j])


def solution(mesh):
    nc, nz = mesh.shape["context"], mesh.shape["tensor"]
    nx = X_CHIPS if nc == 2 * X_CHIPS * X_CHIPS else 2

    def body(tokens_t, qkv_weight, prior_state, norm_gain):
        rows, tokens = tokens_t.shape
        heads = prior_state.shape[0]
        columns = qkv_weight.shape[1]
        tile = heads * HEAD // nc
        width = norm_gain.shape[0] * nz
        any_space = pl.BlockSpec(memory_space=pl.ANY)
        return pl.pallas_call(
            functools.partial(kernel, nc, nx, nz, width),
            out_shape=jax.ShapeDtypeStruct((tokens, heads * HEAD), BF16),
            in_specs=[any_space] * 4,
            out_specs=pl.BlockSpec(memory_space=pltpu.VMEM),
            scratch_shapes=[
                pltpu.VMEM((nz, rows, tokens), BF16),
                pltpu.VMEM((nz, rows, columns), BF16),
                pltpu.VMEM((heads, HEAD, HEAD), F32),
                pltpu.VMEM((1, heads * HEAD), F32),
                pltpu.VMEM((tokens, columns), F32),
                pltpu.VMEM((nc, tile, HEAD), F32),
                pltpu.VMEM((nc, tile, HEAD), F32),
                pltpu.VMEM((nc, tile, HEAD), F32),
                pltpu.VMEM((nc, tile, HEAD), F32),
                pltpu.VMEM((nz, 1, tokens), F32),
                pltpu.SemaphoreType.DMA((2, nz // 2, CHUNKS)),
                pltpu.SemaphoreType.DMA((2, nz // 2 + 1, CHUNKS)),
                pltpu.SemaphoreType.DMA((4,)),
            ]
            + [pltpu.SemaphoreType.DMA] * 6
            + [pltpu.SemaphoreType.REGULAR((4,))],
            compiler_params=pltpu.CompilerParams(
                collective_id=0, has_side_effects=True, vmem_limit_bytes=60 * 1024 * 1024
            ),
        )(
            tokens_t,
            qkv_weight.reshape(nz, rows, columns),
            prior_state,
            norm_gain.reshape(1, -1),
        )

    in_specs = (P("tensor", "context"), P(None, "tensor"), P("tensor", None, None), P("tensor"))
    out_specs = P("context", "tensor")
    return jax.shard_map(body, mesh=mesh, in_specs=in_specs, out_specs=out_specs, check_vma=False)
```

```python
import functools

import jax
import jax.numpy as jnp
from jax import lax
from jax.experimental import pallas as pl
from jax.experimental.pallas import tpu as pltpu
from jax.sharding import PartitionSpec as P

HEAD = 128
EPSILON = 1e-06
CHUNKS = 4
X_CHIPS = 4
F32 = jnp.float32
BF16 = jnp.bfloat16
MESH = pl.DeviceIdType.MESH


def silu(u):
    return u / (1.0 + jnp.exp(-u))


def wait_bytes(ref, sem):
    pltpu.make_async_copy(ref, ref, sem).wait()


def kernel(
    nc, nx, nz, width,
    x_ref, w_ref, prior_ref, gain_ref, out_ref,
    xbuf, wbuf, prior, gain, acc, sbuf, gath, pref, carr, ssq,
    send, recv, local, send1, recv1, send2, recv2, send3, recv3, entered,
):
    ny = nc // (2 * nx)
    half = nz // 2
    rows = xbuf.shape[1]
    piece = rows // CHUNKS
    heads = prior_ref.shape[0]
    c = lax.axis_index("context")
    z = lax.axis_index("tensor")

    px, py, pk = c // (2 * ny), lax.rem(c // 2, ny), lax.rem(c, 2)

    def at_chip(x, y, k):
        return (x * ny + y) * 2 + k

    sibling = at_chip(px, py, 1 - pk)
    along_y = [at_chip(px, lax.rem(py + d, ny), pk) for d in (1, ny - 1)]
    along_x = [at_chip(lax.rem(px + d, nx), py, pk) for d in (1, nx - 1)]

    def signal(sem, to):
        pl.semaphore_signal(sem, inc=1, device_id={"context": to}, device_id_type=MESH)

    own = pltpu.make_async_copy(x_ref, xbuf.at[z], local.at[0])
    weights = pltpu.make_async_copy(w_ref, wbuf, local.at[1])
    prior_in = pltpu.make_async_copy(prior_ref, prior, local.at[2])
    gain_in = pltpu.make_async_copy(gain_ref, gain, local.at[3])

    barrier = pltpu.get_barrier_semaphore()
    for away in (1, 2, nz - 2, nz - 1):
        pl.semaphore_signal(
            barrier, inc=1, device_id={"tensor": lax.rem(z + away, nz)}, device_id_type=MESH
        )
    for to in [sibling] + along_y + along_x:
        signal(barrier, to)
    own.start()
    weights.start()
    prior_in.start()
    gain_in.start()
    pl.semaphore_wait(barrier, 9)

    def source(d, s):
        return lax.rem(z + (nz - s if d == 0 else s), nz)

    def part(j):
        return pl.ds(j * piece, piece)

    def forward(d, s, a, j, src):
        at = source(d, s)
        pltpu.make_async_remote_copy(
            src_ref=src,
            dst_ref=xbuf.at[at, part(j)],
            send_sem=send.at[d, a - 1, j],
            recv_sem=recv.at[d, a, j],
            device_id={"tensor": source(1 - d, a - s)},
            device_id_type=MESH,
        ).start()

    def arrived(d, s, j):
        wait_bytes(xbuf.at[source(d, s), part(j)], recv.at[d, s, j])

    def project(at):
        return lax.dot_general(
            xbuf[at], wbuf[at], (((0,), (0,)), ((), ())), preferred_element_type=F32
        )

    both = [(d, j) for j in range(CHUNKS) for d in range(2)]
    stops, ready = {}, {}
    for d, j in both:
        end = half if (j < CHUNKS // 2) == (d == 0) else half - 1
        stops[d, j] = [0]
        while stops[d, j][-1] < end:
            t, at = len(stops[d, j]) - 1, stops[d, j][-1]
            step = 2 if t % CHUNKS == j and at + 2 <= end else 1
            for between in range(1, step + 1):
                ready[d, at + between, j] = t + 1
            stops[d, j].append(at + step)
    hops = max(len(stop) for stop in stops.values()) - 1

    pending = [(d, a) for a in range(half) for d in range(2 if a else 1)]
    waited = set()

    def need(d, a, j):
        if (d, a, j) not in waited:
            waited.add((d, a, j))
            arrived(d, a, j)

    def gathered(d, a):
        for j in range(CHUNKS if a else 0):
            need(d, a, j)

    def project_one(t):
        if pending:
            d, a = pending[0]
            if max([ready[d, a, j] for j in range(CHUNKS)] if a else [1]) <= t:
                pending.pop(0)
                gathered(d, a)
                if a == 0:
                    own.wait()
                    weights.wait()
                    acc[...] = project(z)
                else:
                    acc[...] += project(source(d, a))

    def greet(t):
        if t == 0:
            for to in along_y:
                signal(entered.at[0], to)
        elif t == 2:
            pl.semaphore_wait(entered.at[0], 2)
            for to in along_x:
                signal(entered.at[1], to)
        elif t == hops - 2:
            pl.semaphore_wait(entered.at[1], 2)
            for to in along_x:
                signal(entered.at[2], to)
        elif t == hops - 1:
            pl.semaphore_wait(entered.at[2], 2)
            signal(entered.at[3], sibling)

    for t in range(hops):
        for group in range(2):
            now = both[group * CHUNKS : (group + 1) * CHUNKS]
            now = [(d, j) for d, j in now if t + 1 < len(stops[d, j])]
            for d, j in now:
                at, to = stops[d, j][t], stops[d, j][t + 1]
                if t:
                    need(d, at, j)
                block = xbuf.at[source(d, at), part(j)] if t else x_ref.at[part(j)]
                forward(d, at, to, j, block)
            for d, j in now:
                at, to = stops[d, j][t], stops[d, j][t + 1]
                if to - at == 2:
                    block = xbuf.at[source(d, at), part(j)] if t else x_ref.at[part(j)]
                    forward(d, at, at + 1, j, block)
            for _ in range(3 if group == 1 and t >= 2 else 0):
                project_one(t - 1)
        greet(t)
    while pending:
        project_one(hops)
    last = source(0, half)
    for d, j in both:
        if stops[d, j][-1] == half:
            need(d, half, j)

    def activated(begin, count):
        span = pl.ds(begin * HEAD, count * HEAD)
        u = acc[:, span] + lax.dot_general(
            xbuf[last], wbuf[last, :, span], (((0,), (0,)), ((), ())), preferred_element_type=F32
        )
        return silu(u).astype(BF16)

    def exchange(h, src, dst, send_sem, recv_sem):
        for dy in sorted(range(ny), key=lambda d: -min(d, ny - d)):
            for x in range(h * nx // heads, (h + 1) * nx // heads):
                for dk in (1, 0):
                    to = at_chip(x, lax.rem(py + dy, ny), pk if dk == 0 else 1 - pk)
                    copy = pltpu.make_async_remote_copy(
                        src_ref=src.at[to],
                        dst_ref=dst.at[c],
                        send_sem=send_sem,
                        recv_sem=recv_sem,
                        device_id={"context": to},
                        device_id_type=MESH,
                    )
                    if dy or dk:
                        copy.start()
                    else:
                        pl.when(px != x)(copy.start)

    others = pl.ds(0, nc - 1)
    keys, values = [], []
    per = nc // heads
    for h in range(heads):
        pair = activated(3 * h + 1, 2)
        keys.append(pair[:, :HEAD])
        values.append(pair[:, HEAD:])
        state = lax.dot_general(
            keys[h], values[h], (((0,), (0,)), ((), ())), preferred_element_type=F32
        )
        sbuf[h * per : (h + 1) * per] = state.reshape(per, HEAD // per, HEAD)
        if h == 0:
            pl.semaphore_wait(entered.at[3], 1)
        exchange(h, sbuf, gath, send1, recv1)
    gath[c] = sbuf[c]

    queries, within = [], []
    tokens = acc.shape[0]
    causal = lax.broadcasted_iota(jnp.int32, (tokens, tokens), 0) >= lax.broadcasted_iota(
        jnp.int32, (tokens, tokens), 1
    )
    for h in range(heads):
        queries.append(activated(3 * h, 1))
        scores = lax.dot_general(
            queries[h], keys[h], (((1,), (1,)), ((), ())), preferred_element_type=F32
        )
        scores = jnp.where(causal, scores, 0.0).astype(BF16)
        within.append(jnp.dot(scores, values[h], preferred_element_type=F32))

    wait_bytes(gath.at[others], recv1)
    running = jnp.zeros(gath.shape[1:], F32)
    for i in range(nc):
        pref[i] = running
        running = running + gath[i]
    for h in range(heads):
        exchange(h, pref, carr, send2, recv2)
    carr[c] = pref[c]
    prior_in.wait()
    gain_in.wait()
    wait_bytes(carr.at[others], recv2)

    attended = []
    for h in range(heads):
        carried = prior[h] + carr[h * per : (h + 1) * per].reshape(HEAD, HEAD)
        high = carried.astype(BF16)
        low = (carried - high.astype(F32)).astype(BF16)
        across = jnp.dot(queries[h], high, preferred_element_type=F32)
        across += jnp.dot(queries[h], low, preferred_element_type=F32)
        attended.append(within[h] + across)
    squares = attended[0] * attended[0]
    for h in range(1, heads):
        squares += attended[h] * attended[h]
    ssq[z] = jnp.sum(squares.T, axis=0, keepdims=True)

    def tell(to):
        pltpu.make_async_remote_copy(
            src_ref=ssq.at[z],
            dst_ref=ssq.at[z],
            send_sem=send3,
            recv_sem=recv3,
            device_id={"tensor": to},
            device_id_type=MESH,
        ).start()

    tell(source(1, half))

    @pl.loop(1, half)
    def _(i):
        tell(source(0, half - i))
        tell(source(1, half - i))

    peers = pl.ds(0, nz - 1)
    wait_bytes(ssq.at[peers], recv3)
    total = jnp.sum(ssq[...], axis=0)
    inverse = lax.rsqrt(total / width + EPSILON)
    column = jnp.broadcast_to(inverse, (HEAD, tokens)).T
    for h in range(heads):
        span = slice(h * HEAD, (h + 1) * HEAD)
        out_ref[:, span] = (attended[h] * column * gain[:, span]).astype(out_ref.dtype)

    wait_bytes(sbuf.at[others], send1)
    wait_bytes(pref.at[others], send2)
    wait_bytes(ssq.at[peers], send3)

    @pl.loop(0, half - 1)
    def _(s):
        for j in range(CHUNKS):
            for d in range(2):
                wait_bytes(xbuf.at[z, part(j)], send.at[d, s, j])

    for j in range(CHUNKS):
        wait_bytes(xbuf.at[z, part(j)], send.at[0 if j < CHUNKS // 2 else 1, half - 1, j])


def solution(mesh):
    nc, nz = mesh.shape["context"], mesh.shape["tensor"]
    nx = X_CHIPS if nc == 2 * X_CHIPS * X_CHIPS else 2

    def body(tokens_t, qkv_weight, prior_state, norm_gain):
        rows, tokens = tokens_t.shape
        heads = prior_state.shape[0]
        columns = qkv_weight.shape[1]
        tile = heads * HEAD // nc
        width = norm_gain.shape[0] * nz
        any_space = pl.BlockSpec(memory_space=pl.ANY)
        return pl.pallas_call(
            functools.partial(kernel, nc, nx, nz, width),
            out_shape=jax.ShapeDtypeStruct((tokens, heads * HEAD), BF16),
            in_specs=[any_space] * 4,
            out_specs=pl.BlockSpec(memory_space=pltpu.VMEM),
            scratch_shapes=[
                pltpu.VMEM((nz, rows, tokens), BF16),
                pltpu.VMEM((nz, rows, columns), BF16),
                pltpu.VMEM((heads, HEAD, HEAD), F32),
                pltpu.VMEM((1, heads * HEAD), F32),
                pltpu.VMEM((tokens, columns), F32),
                pltpu.VMEM((nc, tile, HEAD), F32),
                pltpu.VMEM((nc, tile, HEAD), F32),
                pltpu.VMEM((nc, tile, HEAD), F32),
                pltpu.VMEM((nc, tile, HEAD), F32),
                pltpu.VMEM((nz, 1, tokens), F32),
                pltpu.SemaphoreType.DMA((2, nz // 2, CHUNKS)),
                pltpu.SemaphoreType.DMA((2, nz // 2 + 1, CHUNKS)),
                pltpu.SemaphoreType.DMA((4,)),
            ]
            + [pltpu.SemaphoreType.DMA] * 6
            + [pltpu.SemaphoreType.REGULAR((4,))],
            compiler_params=pltpu.CompilerParams(
                collective_id=0, has_side_effects=True, vmem_limit_bytes=60 * 1024 * 1024
            ),
        )(
            tokens_t,
            qkv_weight.reshape(nz, rows, columns),
            prior_state,
            norm_gain.reshape(1, -1),
        )

    in_specs = (P("tensor", "context"), P(None, "tensor"), P("tensor", None, None), P("tensor"))
    out_specs = P("context", "tensor")
    return jax.shard_map(body, mesh=mesh, in_specs=in_specs, out_specs=out_specs, check_vma=False)
```
